32 devices in a mesh: tm: 4 (over z), rows: 8 (over y, x, core).
Axes of the slice: x: 2, y: 2, z: 4, core: 2. Of those that a mesh axis runs over, the one named last changes fastest.
Arguments:
- frames: bfloat16 [8, 16, 128, 256], P('tm', 'rows'), may hold values from -30 to 30
- frame_counts: int32 [4], replicated, may hold values from 0 to 2, as said below
- norm_gain: float32 [256], replicated, may hold values from 0.5 to 1.5
- norm_bias: float32 [256], replicated, may hold values from -3 to 3
- conv3_weight: bfloat16 [3, 3, 3, 256, 256], replicated, may hold values from -0.078125 to 0.078125
- conv3_bias: float32 [256], replicated, may hold values from -3 to 3
- conv2_weight: bfloat16 [3, 3, 256, 256], replicated, may hold values from -0.125 to 0.125
- conv2_bias: float32 [256], replicated, may hold values from -3 to 3
Outputs:
- decoded: bfloat16 [4, 32, 256, 256], P('tm', 'rows')
The draws below stay inside these ranges and needn't reach their ends.
Inputs may be any that keep to these rules, and one draw needn't show every extreme that they name: `frame_counts`: device d of tm holds the frames starting at the sum of the counts before it, and its first frame index is d or d + 1; the counts sum to 4. Slots at or beyond a device's count hold values that belong to no frame.
All inputs are finite; a program needn't handle non-finite values.
Results may differ from the reference program's by a relative error of at most 0.005.
Values may be sent and summed in bfloat16 or wider, within the bound.
A program may use at most 64 MiB of HBM per device.

```python
import math
import jax
import jax.numpy as jnp
from jax import lax

C = 256
GROUPS = 32
W = 128
FCAP = 2
FRAMES = 4
H = 16
N_TM = 4


def draw_frames(key, part):
    base = jax.random.fold_in(key, 3)
    noise_key, offset_key, channel_key, factor_key, shift_key = jax.random.split(base, 5)
    slot_total = N_TM * FCAP
    full_shape = (slot_total, H, W, C)
    slot_ramp = jnp.arange(slot_total, dtype=jnp.float32) / (slot_total - 1)
    row_ramp = jnp.arange(H, dtype=jnp.float32) / max(H - 1, 1)
    random_level = jax.random.uniform(factor_key, (slot_total, H), jnp.float32, 0.0, 1.0)
    position_scale = jnp.exp(math.log(3.0) * (0.5 * (slot_ramp[:, None] + row_ramp[None, :]) + random_level - 1.0))
    place_offset = jax.random.uniform(shift_key, (slot_total, H), jnp.float32, -1.0, 1.0)
    channel_scale = jnp.exp(jax.random.uniform(channel_key, (C,), jnp.float32, math.log(0.5), math.log(2.0)))
    offsets = jnp.clip(0.5 * jax.random.normal(offset_key, (C,), jnp.float32), -1.5, 1.5)
    noise_field = jnp.clip(jax.random.normal(noise_key, full_shape, jnp.float32), -3.5, 3.5)
    shaped = noise_field * channel_scale + offsets + place_offset[:, :, None, None]
    return (shaped * position_scale[:, :, None, None]).astype(jnp.bfloat16)


def draw_frame_counts(key, part):
    base = jax.random.fold_in(key, 7)
    coin_flips = jax.random.randint(base, (N_TM + 1,), 0, 2)
    boundary = jnp.arange(N_TM + 1)
    lifted = jnp.where((boundary == N_TM - 1) | (boundary == N_TM // 2), 1, coin_flips)
    lifted = jnp.where((boundary == 0) | (boundary == N_TM), 0, lifted)
    return (1 + lifted[1:] - lifted[:-1]).astype(jnp.int32)


def bell_draw(own_key, shape, deviation, limit, kind=jnp.bfloat16):
    values = jax.random.normal(own_key, shape, jnp.float32) * deviation
    return jnp.minimum(jnp.maximum(values, -limit), limit).astype(kind)


def setup_inputs(seed: int = 0) -> dict:
    seeds = jax.random.split(jax.random.key(seed), 9)
    frames = draw_frames(jax.random.fold_in(seeds[8], 71), 0)
    frame_counts = draw_frame_counts(jax.random.fold_in(seeds[8], 71), 0)
    norm_gain = jnp.clip(jax.random.uniform(seeds[2], (C,), jnp.float32, 0.5, 1.5), 0.5, 1.5)
    norm_bias = bell_draw(seeds[3], (C,), 0.5, 3.0, jnp.float32)
    conv3_weight = bell_draw(seeds[4], (3, 3, 3, C, C), (27 * C) ** -0.5, 0.078125)
    conv3_bias = bell_draw(seeds[5], (C,), 0.5, 3.0, jnp.float32)
    conv2_weight = bell_draw(seeds[6], (3, 3, C, C), (9 * C) ** -0.5, 0.125)
    conv2_bias = bell_draw(seeds[7], (C,), 0.5, 3.0, jnp.float32)
    return dict(frames=frames, frame_counts=frame_counts, norm_gain=norm_gain, norm_bias=norm_bias, conv3_weight=conv3_weight, conv3_bias=conv3_bias, conv2_weight=conv2_weight, conv2_bias=conv2_bias)


norm_eps = 1e-06

def reference(frames, frame_counts, norm_gain, norm_bias, conv3_weight, conv3_bias, conv2_weight, conv2_bias):
    starts = (jnp.cumsum(frame_counts) - frame_counts).astype(jnp.int32)
    moments = jnp.arange(FRAMES, dtype=jnp.int32)
    owner_dev = (lax.optimization_barrier(jnp.sum((starts[None, :] <= moments[:, None]).astype(jnp.int32), axis=1)) - 1).astype(jnp.int32)
    position = (owner_dev * FCAP + moments - starts[owner_dev]).astype(jnp.int32)
    clip_frames = frames[position]
    values = clip_frames.astype(jnp.float32)
    grouped = values.reshape(FRAMES, H, W, GROUPS, C // GROUPS)
    group_mean = lax.optimization_barrier(jnp.mean(grouped, axis=(0, 1, 2, 4)))
    group_square = lax.optimization_barrier(jnp.mean(grouped * grouped, axis=(0, 1, 2, 4)))
    inverse = lax.rsqrt(group_square - group_mean * group_mean + norm_eps)
    chan_scale = jnp.repeat(inverse, C // GROUPS) * norm_gain
    chan_shift = norm_bias - jnp.repeat(group_mean * inverse, C // GROUPS) * norm_gain
    hidden = jax.nn.silu(values * chan_scale + chan_shift).astype(jnp.bfloat16)
    padded = jnp.concatenate([hidden[:1], hidden[:1], hidden], axis=0).astype(jnp.float32)
    conv_out = lax.conv_general_dilated(padded[None], conv3_weight.astype(jnp.float32), (1, 1, 1), [(0, 0), (1, 1), (1, 1)], dimension_numbers=('NDHWC', 'DHWIO', 'NDHWC'), precision=lax.Precision.HIGHEST)[0]
    merged = (values + conv_out + conv3_bias).astype(jnp.bfloat16)
    doubled = jnp.repeat(jnp.repeat(merged, 2, axis=1), 2, axis=2).astype(jnp.float32)
    result = lax.conv_general_dilated(doubled, conv2_weight.astype(jnp.float32), (1, 1), [(1, 1), (1, 1)], dimension_numbers=('NHWC', 'HWIO', 'NHWC'), precision=lax.Precision.HIGHEST)
    return (result + conv2_bias).astype(jnp.bfloat16)
```

```python
import functools

import jax
import jax.numpy as jnp
from jax import lax
from jax.experimental import pallas as pl
from jax.experimental.pallas import tpu as pltpu
from jax.sharding import PartitionSpec as P

GROUPS = 32
norm_eps = 1e-06
MESH = pl.DeviceIdType.MESH
f32 = jnp.float32
bf16 = jnp.bfloat16


def roll_rows(value, shift):
    return pltpu.roll(value, shift % value.shape[0], 0)


def side_by_side(value):
    columns = value.shape[0]
    place = lax.broadcasted_iota(jnp.int32, value.shape, 0)
    left = jnp.where(place == 0, 0.0, roll_rows(value, 1))
    right = jnp.where(place == columns - 1, 0.0, roll_rows(value, -1))
    return left, value, right


def group_total(value, width):
    channels = value.shape[1]
    lane = lax.broadcasted_iota(jnp.int32, value.shape, 1)
    step = 1
    while step < width:
        up = pltpu.roll(value, step, 1)
        down = pltpu.roll(value, channels - step, 1)
        value = value + jnp.where((lane // step) % 2 == 1, up, down)
        step *= 2
    return value


def kernel(
    n_tm, n_rows,
    counts, frames, gain, bias, w3_hbm, b3, w2_hbm, b2,
    out,
    w3, w2, cw, xsel, xgot, ext, joined, acc, mjoined, spread,
    mine, row_stats, plane, tm_stats,
    w_sem, sx, rx, sg, rg, sr, rr, s1, r1, s2, r2,
):
    band, columns, channels = frames.shape[1:]
    d = lax.axis_index("tm")
    r = lax.axis_index("rows")

    load3 = pltpu.make_async_copy(w3_hbm, w3, w_sem.at[0])
    load2 = pltpu.make_async_copy(w2_hbm, w2, w_sem.at[1])
    load2.start()
    load3.start()

    barrier = pltpu.get_barrier_semaphore()
    for k in range(1, n_rows):
        pl.semaphore_signal(
            barrier, inc=1, device_id={"rows": lax.rem(r + k, n_rows)}, device_id_type=MESH
        )
    for k in range(1, n_tm):
        pl.semaphore_signal(
            barrier, inc=1, device_id={"tm": lax.rem(d + k, n_tm)}, device_id_type=MESH
        )

    start = jnp.int32(0)
    for i in range(n_tm):
        start = start + jnp.where(i < d, counts[i], 0)
    live = counts[d]
    own_first = start == d

    for row in range(band):
        xsel[row] = jnp.where(own_first, frames[1, row], frames[0, row])
    total = jnp.zeros((8, channels), f32)
    square = jnp.zeros((8, channels), f32)
    for slot in range(frames.shape[0]):
        for row in range(band):
            value = jnp.where(slot < live, frames[slot, row].astype(f32), 0.0)
            value = value.reshape(columns // 8, 8, channels)
            total = total + jnp.sum(value, axis=0)
            square = square + jnp.sum(value * value, axis=0)
    total = jnp.sum(total, axis=0, keepdims=True)
    square = jnp.sum(square, axis=0, keepdims=True)
    mine[...] = jnp.concatenate(
        [jnp.broadcast_to(total, (4, channels)), jnp.broadcast_to(square, (4, channels))], axis=0
    )
    pl.semaphore_wait(barrier, n_rows - 1 + n_tm - 1)

    def x_copy(row):
        return pltpu.make_async_remote_copy(
            src_ref=xsel.at[row], dst_ref=xgot.at[row], send_sem=sx.at[row], recv_sem=rx.at[row],
            device_id={"tm": lax.rem(d + 1, n_tm)}, device_id_type=MESH,
        )

    def g_copy(frame, row):
        return pltpu.make_async_remote_copy(
            src_ref=ext.at[frame, band + row], dst_ref=ext.at[frame - 1, band + row],
            send_sem=sg.at[frame - 1, row], recv_sem=rg.at[frame - 1, row],
            device_id={"tm": lax.rem(d + 1, n_tm)}, device_id_type=MESH,
        )

    def r_copy(frame, row, down):
        target = lax.rem(r + (1 if down else n_rows - 1), n_rows)
        return pltpu.make_async_remote_copy(
            src_ref=ext.at[frame, band + row],
            dst_ref=ext.at[frame, (0 if down else 2 * band) + row],
            send_sem=sr.at[frame, row, down], recv_sem=rr.at[frame, row, down],
            device_id={"rows": target}, device_id_type=MESH,
        )

    has_next, has_last = d < n_tm - 1, d > 0
    has_above, has_below = r > 0, r < n_rows - 1
    edge_up = range(2)
    edge_down = range(band - 2, band)

    def stat1(k):
        return pltpu.make_async_remote_copy(
            src_ref=mine, dst_ref=row_stats.at[k - 1], send_sem=s1.at[k - 1], recv_sem=r1.at[k - 1],
            device_id={"rows": lax.rem(r + k, n_rows)}, device_id_type=MESH,
        )

    def stat2(k):
        return pltpu.make_async_remote_copy(
            src_ref=plane, dst_ref=tm_stats.at[k - 1], send_sem=s2.at[k - 1], recv_sem=r2.at[k - 1],
            device_id={"tm": lax.rem(d + k, n_tm)}, device_id_type=MESH,
        )

    for k in range(1, n_rows):
        stat1(k).start()

    @pl.when(has_next)
    def _():
        for row in range(band):
            x_copy(row).start()

    load2.wait()
    for phase_row in range(2):
        for tap_row in range(2):
            for phase_col in range(2):
                for tap_col in range(2):
                    rows_of = ((0,), (1, 2)) if phase_row == 0 else ((0, 1), (2,))
                    cols_of = ((0,), (1, 2)) if phase_col == 0 else ((0, 1), (2,))
                    summed = None
                    for a in rows_of[tap_row]:
                        for b in cols_of[tap_col]:
                            part = w2[a, b].astype(f32)
                            summed = part if summed is None else summed + part
                    cw[phase_row, tap_row, phase_col, pl.ds(tap_col * channels, channels), :] = (
                        summed.astype(bf16)
                    )

    for k in range(1, n_rows):
        stat1(k).wait_recv()
    plane_sum = mine[...]
    for k in range(1, n_rows):
        plane_sum = plane_sum + row_stats[k - 1]
    plane[...] = plane_sum

    def send_rows(frame, row):
        @pl.when(has_above)
        def _():
            if row in edge_up:
                r_copy(frame, row, 0).start()

        @pl.when(has_below)
        def _():
            if row in edge_down:
                r_copy(frame, row, 1).start()

    for row in range(band):
        @pl.when(has_last)
        def _():
            x_copy(row).wait_recv()
            ext[2, band + row] = jnp.where(own_first, frames[0, row], xgot[row])

        @pl.when(d == 0)
        def _():
            ext[2, band + row] = frames[0, row]
            ext[1, band + row] = frames[0, row]
            ext[0, band + row] = frames[0, row]

        if row == 0:
            for k in range(1, n_tm):
                stat2(k).start()

        @pl.when(has_next)
        def _():
            g_copy(2, row).start()

        send_rows(2, row)

    for row in range(band):
        @pl.when(has_last)
        def _():
            g_copy(2, row).wait_recv()

        @pl.when(has_next)
        def _():
            g_copy(1, row).start()

        send_rows(1, row)

    for k in range(1, n_tm):
        stat2(k).wait_recv()
    whole = plane[...]
    for k in range(1, n_tm):
        whole = whole + tm_stats[k - 1]
    width = channels // GROUPS
    whole = group_total(whole, width) / float(n_tm * n_rows * band * columns * width)
    mean, mean_square = whole[0:1], whole[4:5]
    inverse = lax.rsqrt(mean_square - mean * mean + norm_eps)
    scale = inverse * gain[...]
    shift = bias[...] - mean * inverse * gain[...]

    def hide(frame, j):
        value = ext[frame, band - 2 + j].astype(f32) * scale + shift
        value = 0.5 * value * (1.0 + jnp.tanh(0.5 * value))
        place = r * band + j - 2
        value = jnp.where((place >= 0) & (place < n_rows * band), value, 0.0)
        for i, part in enumerate(side_by_side(value)):
            joined[frame, pl.ds(j * columns, columns), pl.ds(i * channels, channels)] = (
                part.astype(bf16)
            )

    def wait_rows(frame):
        @pl.when(has_below)
        def _():
            for row in edge_up:
                r_copy(frame, row, 0).wait_recv()

        @pl.when(has_above)
        def _():
            for row in edge_down:
                r_copy(frame, row, 1).wait_recv()

    def taps(frame):
        depth = (band + 2) * columns
        summed = None
        for k in range(3):
            part = jnp.dot(
                joined[frame, pl.ds(k * columns, depth), :], w3[frame, k],
                preferred_element_type=f32,
            )
            summed = part if summed is None else summed + part
        return summed

    own = range(2, band + 2)
    halo = [j for j in range(band + 4) if j not in own]

    for j in own:
        hide(2, j)
    for j in own:
        hide(1, j)
    for row in range(band):
        @pl.when(has_last)
        def _():
            g_copy(1, row).wait_recv()

        send_rows(0, row)
    wait_rows(2)
    for j in halo:
        hide(2, j)
    load3.wait()
    acc[...] = taps(2)
    for j in own:
        hide(0, j)
    wait_rows(1)
    for j in halo:
        hide(1, j)
    acc[...] += taps(1)
    wait_rows(0)
    for j in halo:
        hide(0, j)
    acc[...] += taps(0)

    for j in range(band + 2):
        value = ext[2, band - 1 + j].astype(f32) + acc[pl.ds(j * columns, columns), :] + b3[...]
        place = r * band + j - 1
        value = jnp.where((place >= 0) & (place < n_rows * band), value, 0.0)
        for i, part in enumerate(side_by_side(value)):
            mjoined[pl.ds(j * columns, columns), pl.ds(i * channels, channels)] = part.astype(bf16)

    for p in range(2):
        for q in range(2):
            summed = b2[...]
            for t in range(2):
                summed = summed + jnp.dot(
                    mjoined[pl.ds((p + t) * columns, band * columns), pl.ds(q * channels, 2 * channels)],
                    cw[p, t, q], preferred_element_type=f32,
                )
            for i in range(band):
                for lane in range(0, channels, 128):
                    spread[2 * i + p, lane // 128, pl.ds(q, columns, stride=2), :] = (
                        summed[i * columns : (i + 1) * columns, lane : lane + 128]
                    )
        for i in range(band):
            for lane in range(0, channels, 128):
                out[2 * i + p, :, pl.ds(lane, 128)] = spread[2 * i + p, lane // 128].astype(bf16)

    for k in range(1, n_rows):
        stat1(k).wait_send()
    for k in range(1, n_tm):
        stat2(k).wait_send()

    @pl.when(has_next)
    def _():
        for row in range(band):
            x_copy(row).wait_send()
            g_copy(2, row).wait_send()
            g_copy(1, row).wait_send()

    @pl.when(has_above)
    def _():
        for frame in range(3):
            for row in edge_up:
                r_copy(frame, row, 0).wait_send()

    @pl.when(has_below)
    def _():
        for frame in range(3):
            for row in edge_down:
                r_copy(frame, row, 1).wait_send()


def body(
    frames, frame_counts, norm_gain, norm_bias, conv3_weight, conv3_bias, conv2_weight, conv2_bias
):
    n_tm, n_rows = lax.axis_size("tm"), lax.axis_size("rows")
    _, band, columns, channels = frames.shape
    vmem = pl.BlockSpec(memory_space=pltpu.VMEM)
    anywhere = pl.BlockSpec(memory_space=pl.ANY)
    dma = pltpu.SemaphoreType.DMA
    return pl.pallas_call(
        functools.partial(kernel, n_tm, n_rows),
        out_shape=jax.ShapeDtypeStruct((1, 2 * band, 2 * columns, channels), bf16),
        in_specs=[
            pl.BlockSpec(memory_space=pltpu.SMEM), vmem, vmem, vmem, anywhere, vmem, anywhere, vmem
        ],
        out_specs=pl.BlockSpec((None, 2 * band, 2 * columns, channels), lambda: (0, 0, 0, 0)),
        scratch_shapes=[
            pltpu.VMEM((3, 3, 3 * channels, channels), bf16),
            pltpu.VMEM((3, 3, channels, channels), bf16),
            pltpu.VMEM((2, 2, 2, 2 * channels, channels), bf16),
            pltpu.VMEM((band, columns, channels), bf16),
            pltpu.VMEM((band, columns, channels), bf16),
            pltpu.VMEM((3, 3 * band, columns, channels), bf16),
            pltpu.VMEM((3, (band + 4) * columns, 3 * channels), bf16),
            pltpu.VMEM(((band + 2) * columns, channels), f32),
            pltpu.VMEM(((band + 2) * columns, 3 * channels), bf16),
            pltpu.VMEM((2 * band, channels // 128, 2 * columns, 128), f32),
            pltpu.VMEM((8, channels), f32),
            pltpu.VMEM((n_rows - 1, 8, channels), f32),
            pltpu.VMEM((8, channels), f32),
            pltpu.VMEM((n_tm - 1, 8, channels), f32),
            dma((2,)),
            dma((band,)), dma((band,)),
            dma((2, band)), dma((2, band)),
            dma((3, band, 2)), dma((3, band, 2)),
            dma((n_rows - 1,)), dma((n_rows - 1,)),
            dma((n_tm - 1,)), dma((n_tm - 1,)),
        ],
        compiler_params=pltpu.CompilerParams(collective_id=0, has_side_effects=True),
        name="decoder_section",
    )(
        frame_counts, frames, norm_gain[None], norm_bias[None],
        conv3_weight.reshape(3, 3, 3 * channels, channels), conv3_bias[None],
        conv2_weight, conv2_bias[None],
    )


def solution(mesh):
    placed = (P("tm", "rows", None, None), P(), P(), P(), P(), P(), P(), P())
    return jax.shard_map(
        body, mesh=mesh, in_specs=placed, out_specs=P("tm", "rows", None, None), check_vma=False
    )
```

```python
import functools

import jax
import jax.numpy as jnp
from jax import lax
from jax.experimental import pallas as pl
from jax.experimental.pallas import tpu as pltpu
from jax.sharding import PartitionSpec as P

GROUPS = 32
norm_eps = 1e-06
MESH = pl.DeviceIdType.MESH
f32 = jnp.float32
bf16 = jnp.bfloat16


def roll_rows(value, shift):
    return pltpu.roll(value, shift % value.shape[0], 0)


def side_by_side(value):
    columns = value.shape[0]
    place = lax.broadcasted_iota(jnp.int32, value.shape, 0)
    left = jnp.where(place == 0, 0.0, roll_rows(value, 1))
    right = jnp.where(place == columns - 1, 0.0, roll_rows(value, -1))
    return left, value, right


def group_total(value, width):
    channels = value.shape[1]
    lane = lax.broadcasted_iota(jnp.int32, value.shape, 1)
    step = 1
    while step < width:
        up = pltpu.roll(value, step, 1)
        down = pltpu.roll(value, channels - step, 1)
        value = value + jnp.where((lane // step) % 2 == 1, up, down)
        step *= 2
    return value


def kernel(
    n_tm, n_rows,
    counts_hbm, frames_hbm, gain_hbm, bias_hbm, w3_hbm, b3_hbm, w2_hbm, b2_hbm,
    out,
    counts, frames, gain, bias, b3, b2,
    w3, w2, cw, xsel, xgot, ext, joined, acc, mjoined, spread,
    mine, row_stats, plane, tm_stats,
    w_sem, sx, rx, sg, rg, sr, rr, s1, r1, s2, r2,
):
    band, columns, channels = frames_hbm.shape[1:]
    d = lax.axis_index("tm")
    r = lax.axis_index("rows")

    barrier = pltpu.get_barrier_semaphore()
    for k in range(1, n_rows):
        pl.semaphore_signal(
            barrier, inc=1, device_id={"rows": lax.rem(r + k, n_rows)}, device_id_type=MESH
        )
    for k in range(1, n_tm):
        pl.semaphore_signal(
            barrier, inc=1, device_id={"tm": lax.rem(d + k, n_tm)}, device_id_type=MESH
        )

    load_counts = pltpu.make_async_copy(counts_hbm, counts, w_sem.at[2])
    load_frames = pltpu.make_async_copy(frames_hbm, frames, w_sem.at[3])
    load3 = pltpu.make_async_copy(w3_hbm, w3, w_sem.at[0])
    load2 = pltpu.make_async_copy(w2_hbm, w2, w_sem.at[1])
    small = [
        pltpu.make_async_copy(source, target, w_sem.at[4 + i])
        for i, (source, target) in enumerate(
            ((gain_hbm, gain), (bias_hbm, bias), (b3_hbm, b3), (b2_hbm, b2))
        )
    ]
    load_counts.start()
    load_frames.start()
    load2.start()
    load3.start()
    for load in small:
        load.start()
    load_counts.wait()
    load_frames.wait()

    start = jnp.int32(0)
    for i in range(n_tm):
        start = start + jnp.where(i < d, counts[i], 0)
    live = counts[d]
    own_first = start == d

    for row in range(band):
        xsel[row] = jnp.where(own_first, frames[1, row], frames[0, row])
    pl.semaphore_wait(barrier, n_rows - 1 + n_tm - 1)

    def x_copy(row):
        return pltpu.make_async_remote_copy(
            src_ref=xsel.at[row], dst_ref=xgot.at[row], send_sem=sx.at[row], recv_sem=rx.at[row],
            device_id={"tm": lax.rem(d + 1, n_tm)}, device_id_type=MESH,
        )

    def g_copy(frame, row):
        return pltpu.make_async_remote_copy(
            src_ref=ext.at[frame, band + row], dst_ref=ext.at[frame - 1, band + row],
            send_sem=sg.at[frame - 1, row], recv_sem=rg.at[frame - 1, row],
            device_id={"tm": lax.rem(d + 1, n_tm)}, device_id_type=MESH,
        )

    def r_copy(frame, row, down):
        target = lax.rem(r + (1 if down else n_rows - 1), n_rows)
        return pltpu.make_async_remote_copy(
            src_ref=ext.at[frame, band + row],
            dst_ref=ext.at[frame, (0 if down else 2 * band) + row],
            send_sem=sr.at[frame, row, down], recv_sem=rr.at[frame, row, down],
            device_id={"rows": target}, device_id_type=MESH,
        )

    has_next, has_last = d < n_tm - 1, d > 0
    has_above, has_below = r > 0, r < n_rows - 1
    edge_up = range(2)
    edge_down = range(band - 2, band)

    def stat1(k):
        return pltpu.make_async_remote_copy(
            src_ref=mine, dst_ref=row_stats.at[k - 1], send_sem=s1.at[k - 1], recv_sem=r1.at[k - 1],
            device_id={"rows": lax.rem(r + k, n_rows)}, device_id_type=MESH,
        )

    def stat2(k):
        return pltpu.make_async_remote_copy(
            src_ref=plane, dst_ref=tm_stats.at[k - 1], send_sem=s2.at[k - 1], recv_sem=r2.at[k - 1],
            device_id={"tm": lax.rem(d + k, n_tm)}, device_id_type=MESH,
        )

    @pl.when(has_next)
    def _():
        for row in range(band):
            x_copy(row).start()

    total = jnp.zeros((8, channels), f32)
    square = jnp.zeros((8, channels), f32)
    for slot in range(frames_hbm.shape[0]):
        for row in range(band):
            value = jnp.where(slot < live, frames[slot, row].astype(f32), 0.0)
            value = value.reshape(columns // 8, 8, channels)
            total = total + jnp.sum(value, axis=0)
            square = square + jnp.sum(value * value, axis=0)
    total = jnp.sum(total, axis=0, keepdims=True)
    square = jnp.sum(square, axis=0, keepdims=True)
    mine[...] = jnp.concatenate(
        [jnp.broadcast_to(total, (4, channels)), jnp.broadcast_to(square, (4, channels))], axis=0
    )
    for k in range(1, n_rows):
        stat1(k).start()

    load2.wait()
    for phase_row in range(2):
        for tap_row in range(2):
            for phase_col in range(2):
                for tap_col in range(2):
                    rows_of = ((0,), (1, 2)) if phase_row == 0 else ((0, 1), (2,))
                    cols_of = ((0,), (1, 2)) if phase_col == 0 else ((0, 1), (2,))
                    summed = None
                    for a in rows_of[tap_row]:
                        for b in cols_of[tap_col]:
                            part = w2[a, b].astype(f32)
                            summed = part if summed is None else summed + part
                    cw[phase_row, tap_row, phase_col, pl.ds(tap_col * channels, channels), :] = (
                        summed.astype(bf16)
                    )

    def send_rows(frame, row):
        @pl.when(has_above)
        def _():
            if row in edge_up:
                r_copy(frame, row, 0).start()

        @pl.when(has_below)
        def _():
            if row in edge_down:
                r_copy(frame, row, 1).start()

    for row in range(band):
        @pl.when(has_last)
        def _():
            x_copy(row).wait_recv()
            ext[2, band + row] = jnp.where(own_first, frames[0, row], xgot[row])

        @pl.when(d == 0)
        def _():
            ext[2, band + row] = frames[0, row]
            ext[1, band + row] = frames[0, row]
            ext[0, band + row] = frames[0, row]

        @pl.when(has_next)
        def _():
            g_copy(2, row).start()

        send_rows(2, row)

        if row == 0:
            for k in range(1, n_rows):
                stat1(k).wait_recv()
            plane_sum = mine[...]
            for k in range(1, n_rows):
                plane_sum = plane_sum + row_stats[k - 1]
            plane[...] = plane_sum
            for k in range(1, n_tm):
                stat2(k).start()

    for row in range(band):
        @pl.when(has_last)
        def _():
            g_copy(2, row).wait_recv()

        @pl.when(has_next)
        def _():
            g_copy(1, row).start()

        send_rows(1, row)

    for k in range(1, n_tm):
        stat2(k).wait_recv()
    whole = plane[...]
    for k in range(1, n_tm):
        whole = whole + tm_stats[k - 1]
    width = channels // GROUPS
    whole = group_total(whole, width) / float(n_tm * n_rows * band * columns * width)
    mean, mean_square = whole[0:1], whole[4:5]
    inverse = lax.rsqrt(mean_square - mean * mean + norm_eps)
    for load in small:
        load.wait()
    scale = inverse * gain[...]
    shift = bias[...] - mean * inverse * gain[...]

    def slot_of(j):
        return j - 2 if 2 <= j < band + 2 else j + band if j < 2 else j

    def hide(frame, j):
        value = ext[frame, band - 2 + j].astype(f32) * scale + shift
        value = 0.5 * value * (1.0 + jnp.tanh(0.5 * value))
        place = r * band + j - 2
        value = jnp.where((place >= 0) & (place < n_rows * band), value, 0.0)
        for i, part in enumerate(side_by_side(value)):
            joined[frame, pl.ds(slot_of(j) * columns, columns), pl.ds(i * channels, channels)] = (
                part.astype(bf16)
            )

    def wait_rows(frame):
        @pl.when(has_below)
        def _():
            for row in edge_up:
                r_copy(frame, row, 0).wait_recv()

        @pl.when(has_above)
        def _():
            for row in edge_down:
                r_copy(frame, row, 1).wait_recv()

    def tap(frame, k, first, rows):
        return jnp.dot(
            joined[frame, pl.ds(first * columns, rows * columns), :], w3[frame, k],
            preferred_element_type=f32,
        )

    def own_taps(frame):
        for k in range(3):
            acc[pl.ds((2 - k) * columns, band * columns), :] += tap(frame, k, 0, band)

    def halo_taps(frame):
        acc[pl.ds(0, 2 * columns), :] += tap(frame, 0, band, 2)
        acc[pl.ds(band * columns, 2 * columns), :] += tap(frame, 2, band + 2, 2)
        middle = tap(frame, 1, band + 1, 2)
        acc[pl.ds(0, columns), :] += middle[:columns]
        acc[pl.ds((band + 1) * columns, columns), :] += middle[columns:]

    own = range(2, band + 2)
    halo = [j for j in range(band + 4) if j not in own]

    def hide_rows(frame, rows):
        for j in rows:
            hide(frame, j)

    def older(row):
        @pl.when(has_last)
        def _():
            g_copy(1, row).wait_recv()

        send_rows(0, row)

    acc[...] = jnp.zeros(acc.shape, f32) + b3[...]
    hide_rows(2, own)
    load3.wait()
    own_taps(2)
    hide_rows(1, own)
    older(0)
    wait_rows(2)
    hide_rows(2, halo)
    halo_taps(2)
    for row in range(1, band):
        older(row)
    own_taps(1)
    hide_rows(0, own)
    wait_rows(1)
    hide_rows(1, halo)
    halo_taps(1)
    own_taps(0)
    wait_rows(0)
    hide_rows(0, halo)
    halo_taps(0)

    for j in range(band + 2):
        value = ext[2, band - 1 + j].astype(f32) + acc[pl.ds(j * columns, columns), :]
        place = r * band + j - 1
        value = jnp.where((place >= 0) & (place < n_rows * band), value, 0.0)
        for i, part in enumerate(side_by_side(value)):
            mjoined[pl.ds(j * columns, columns), pl.ds(i * channels, channels)] = part.astype(bf16)

    for p in range(2):
        for q in range(2):
            summed = b2[...]
            for t in range(2):
                summed = summed + jnp.dot(
                    mjoined[pl.ds((p + t) * columns, band * columns), pl.ds(q * channels, 2 * channels)],
                    cw[p, t, q], preferred_element_type=f32,
                )
            for i in range(band):
                for lane in range(0, channels, 128):
                    spread[2 * i + p, lane // 128, pl.ds(q, columns, stride=2), :] = (
                        summed[i * columns : (i + 1) * columns, lane : lane + 128]
                    )
        for i in range(band):
            for lane in range(0, channels, 128):
                out[0, 2 * i + p, :, pl.ds(lane, 128)] = spread[2 * i + p, lane // 128].astype(bf16)

    for k in range(1, n_rows):
        stat1(k).wait_send()
    for k in range(1, n_tm):
        stat2(k).wait_send()

    @pl.when(has_next)
    def _():
        for row in range(band):
            x_copy(row).wait_send()
            g_copy(2, row).wait_send()
            g_copy(1, row).wait_send()

    @pl.when(has_above)
    def _():
        for frame in range(3):
            for row in edge_up:
                r_copy(frame, row, 0).wait_send()

    @pl.when(has_below)
    def _():
        for frame in range(3):
            for row in edge_down:
                r_copy(frame, row, 1).wait_send()


def body(
    frames, frame_counts, norm_gain, norm_bias, conv3_weight, conv3_bias, conv2_weight, conv2_bias
):
    n_tm, n_rows = lax.axis_size("tm"), lax.axis_size("rows")
    _, band, columns, channels = frames.shape
    vmem = pl.BlockSpec(memory_space=pltpu.VMEM)
    hbm = pl.BlockSpec(memory_space=pltpu.HBM)
    dma = pltpu.SemaphoreType.DMA
    return pl.pallas_call(
        functools.partial(kernel, n_tm, n_rows),
        out_shape=pltpu.VMEM((1, 2 * band, 2 * columns, channels), bf16),
        in_specs=[
            hbm
        ] * 8,
        out_specs=vmem,
        scratch_shapes=[
            pltpu.SMEM((n_tm,), jnp.int32),
            pltpu.VMEM(frames.shape, bf16),
            pltpu.VMEM((1, channels), f32),
            pltpu.VMEM((1, channels), f32),
            pltpu.VMEM((1, channels), f32),
            pltpu.VMEM((1, channels), f32),
            pltpu.VMEM((3, 3, 3 * channels, channels), bf16),
            pltpu.VMEM((3, 3, channels, channels), bf16),
            pltpu.VMEM((2, 2, 2, 2 * channels, channels), bf16),
            pltpu.VMEM((band, columns, channels), bf16),
            pltpu.VMEM((band, columns, channels), bf16),
            pltpu.VMEM((3, 3 * band, columns, channels), bf16),
            pltpu.VMEM((3, (band + 4) * columns, 3 * channels), bf16),
            pltpu.VMEM(((band + 2) * columns, channels), f32),
            pltpu.VMEM(((band + 2) * columns, 3 * channels), bf16),
            pltpu.VMEM((2 * band, channels // 128, 2 * columns, 128), f32),
            pltpu.VMEM((8, channels), f32),
            pltpu.VMEM((n_rows - 1, 8, channels), f32),
            pltpu.VMEM((8, channels), f32),
            pltpu.VMEM((n_tm - 1, 8, channels), f32),
            dma((8,)),
            dma((band,)), dma((band,)),
            dma((2, band)), dma((2, band)),
            dma((3, band, 2)), dma((3, band, 2)),
            dma((n_rows - 1,)), dma((n_rows - 1,)),
            dma((n_tm - 1,)), dma((n_tm - 1,)),
        ],
        compiler_params=pltpu.CompilerParams(
            collective_id=0, has_side_effects=True, vmem_limit_bytes=60000000
        ),
        name="decoder_section",
    )(
        frame_counts, frames, norm_gain[None], norm_bias[None],
        conv3_weight.reshape(3, 3, 3 * channels, channels), conv3_bias[None],
        conv2_weight, conv2_bias[None],
    )


def solution(mesh):
    placed = (P("tm", "rows", None, None), P(), P(), P(), P(), P(), P(), P())
    return jax.shard_map(
        body, mesh=mesh, in_specs=placed, out_specs=P("tm", "rows", None, None), check_vma=False
    )
```

```python
import functools

import jax
import jax.numpy as jnp
from jax import lax
from jax.experimental import pallas as pl
from jax.experimental.pallas import tpu as pltpu
from jax.sharding import PartitionSpec as P

GROUPS = 32
norm_eps = 1e-06
HALVES = 2
MESH = pl.DeviceIdType.MESH
f32 = jnp.float32
bf16 = jnp.bfloat16


def roll_rows(value, shift):
    return pltpu.roll(value, shift % value.shape[0], 0)


def side_by_side(value):
    columns = value.shape[0]
    place = lax.broadcasted_iota(jnp.int32, value.shape, 0)
    left = jnp.where(place == 0, 0.0, roll_rows(value, 1))
    right = jnp.where(place == columns - 1, 0.0, roll_rows(value, -1))
    return left, value, right


def group_total(value, width):
    channels = value.shape[1]
    lane = lax.broadcasted_iota(jnp.int32, value.shape, 1)
    step = 1
    while step < width:
        up = pltpu.roll(value, step, 1)
        down = pltpu.roll(value, channels - step, 1)
        value = value + jnp.where((lane // step) % 2 == 1, up, down)
        step *= 2
    return value


def kernel(
    n_tm, n_rows,
    counts_hbm, frames_hbm, gain_hbm, bias_hbm, w3_hbm, b3_hbm, w2_hbm, b2_hbm,
    out,
    counts, frames, gain, bias, b3, b2,
    w3, w2, cw, xsel, xgot, ext, joined, acc, mjoined, spread,
    mine, row_stats, plane, tm_stats,
    w_sem, sx, rx, sg, rg, sr, rr, s1, r1, s2, r2,
):
    band, columns, channels = frames_hbm.shape[1:]
    halves = HALVES if columns % (16 * HALVES) == 0 else 1
    span = columns // halves
    chunks = range(band * halves)
    d = lax.axis_index("tm")
    r = lax.axis_index("rows")

    barrier = pltpu.get_barrier_semaphore()
    for k in range(1, n_rows):
        pl.semaphore_signal(
            barrier, inc=1, device_id={"rows": lax.rem(r + k, n_rows)}, device_id_type=MESH
        )
    for k in range(1, n_tm):
        pl.semaphore_signal(
            barrier, inc=1, device_id={"tm": lax.rem(d + k, n_tm)}, device_id_type=MESH
        )

    load_counts = pltpu.make_async_copy(counts_hbm, counts, w_sem.at[2])
    load_frames = pltpu.make_async_copy(frames_hbm, frames, w_sem.at[3])
    load3 = pltpu.make_async_copy(w3_hbm, w3, w_sem.at[0])
    load2 = pltpu.make_async_copy(w2_hbm, w2, w_sem.at[1])
    small = [
        pltpu.make_async_copy(source, target, w_sem.at[4 + i])
        for i, (source, target) in enumerate(
            ((gain_hbm, gain), (bias_hbm, bias), (b3_hbm, b3), (b2_hbm, b2))
        )
    ]
    load_counts.start()
    load_frames.start()
    load2.start()
    load3.start()
    for load in small:
        load.start()
    load_counts.wait()
    load_frames.wait()

    start = jnp.int32(0)
    for i in range(n_tm):
        start = start + jnp.where(i < d, counts[i], 0)
    live = counts[d]
    own_first = start == d

    for row in range(band):
        xsel[row] = jnp.where(own_first, frames[1, row], frames[0, row])
    pl.semaphore_wait(barrier, n_rows - 1 + n_tm - 1)

    def piece(ref, row, chunk):
        return ref.at[row + chunk // halves, pl.ds(chunk % halves * span, span)]

    def x_copy(chunk):
        return pltpu.make_async_remote_copy(
            src_ref=piece(xsel, 0, chunk), dst_ref=piece(xgot, 0, chunk),
            send_sem=sx.at[chunk], recv_sem=rx.at[chunk],
            device_id={"tm": lax.rem(d + 1, n_tm)}, device_id_type=MESH,
        )

    def g_copy(frame, chunk):
        return pltpu.make_async_remote_copy(
            src_ref=piece(ext.at[frame], band, chunk), dst_ref=piece(ext.at[frame - 1], band, chunk),
            send_sem=sg.at[frame - 1, chunk], recv_sem=rg.at[frame - 1, chunk],
            device_id={"tm": lax.rem(d + 1, n_tm)}, device_id_type=MESH,
        )

    def r_copy(frame, chunk, down):
        target = lax.rem(r + (1 if down else n_rows - 1), n_rows)
        return pltpu.make_async_remote_copy(
            src_ref=piece(ext.at[frame], band, chunk),
            dst_ref=piece(ext.at[frame], 0 if down else 2 * band, chunk),
            send_sem=sr.at[frame, chunk, down], recv_sem=rr.at[frame, chunk, down],
            device_id={"rows": target}, device_id_type=MESH,
        )

    has_next, has_last = d < n_tm - 1, d > 0
    has_above, has_below = r > 0, r < n_rows - 1
    edge_up = range(2 * halves)
    edge_down = range((band - 2) * halves, band * halves)

    def stat1(k):
        return pltpu.make_async_remote_copy(
            src_ref=mine, dst_ref=row_stats.at[k - 1], send_sem=s1.at[k - 1], recv_sem=r1.at[k - 1],
            device_id={"rows": lax.rem(r + k, n_rows)}, device_id_type=MESH,
        )

    def stat2(k):
        return pltpu.make_async_remote_copy(
            src_ref=plane, dst_ref=tm_stats.at[k - 1], send_sem=s2.at[k - 1], recv_sem=r2.at[k - 1],
            device_id={"tm": lax.rem(d + k, n_tm)}, device_id_type=MESH,
        )

    @pl.when(has_next)
    def _():
        for chunk in chunks:
            x_copy(chunk).start()

    total = jnp.zeros((8, channels), f32)
    square = jnp.zeros((8, channels), f32)
    for slot in range(frames_hbm.shape[0]):
        for row in range(band):
            value = jnp.where(slot < live, frames[slot, row].astype(f32), 0.0)
            value = value.reshape(columns // 8, 8, channels)
            total = total + jnp.sum(value, axis=0)
            square = square + jnp.sum(value * value, axis=0)
    total = jnp.sum(total, axis=0, keepdims=True)
    square = jnp.sum(square, axis=0, keepdims=True)
    mine[...] = jnp.concatenate(
        [total, square], axis=0
    )
    for k in range(1, n_rows):
        stat1(k).start()

    load2.wait()
    for phase_row in range(2):
        for tap_row in range(2):
            for phase_col in range(2):
                for tap_col in range(2):
                    rows_of = ((0,), (1, 2)) if phase_row == 0 else ((0, 1), (2,))
                    cols_of = ((0,), (1, 2)) if phase_col == 0 else ((0, 1), (2,))
                    summed = None
                    for a in rows_of[tap_row]:
                        for b in cols_of[tap_col]:
                            part = w2[a, b].astype(f32)
                            summed = part if summed is None else summed + part
                    cw[phase_row, tap_row, phase_col, pl.ds(tap_col * channels, channels), :] = (
                        summed.astype(bf16)
                    )

    def send_rows(frame, chunk):
        @pl.when(has_above)
        def _():
            if chunk in edge_up:
                r_copy(frame, chunk, 0).start()

        @pl.when(has_below)
        def _():
            if chunk in edge_down:
                r_copy(frame, chunk, 1).start()

    for chunk in chunks:
        row, cells = chunk // halves, pl.ds(chunk % halves * span, span)

        @pl.when(has_last)
        def _():
            x_copy(chunk).wait_recv()
            ext[2, band + row, cells] = jnp.where(own_first, frames[0, row, cells], xgot[row, cells])

        @pl.when(d == 0)
        def _():
            for frame in range(3):
                ext[frame, band + row, cells] = frames[0, row, cells]

        @pl.when(has_next)
        def _():
            g_copy(2, chunk).start()

        send_rows(2, chunk)

        if chunk == halves - 1:
            for k in range(1, n_rows):
                stat1(k).wait_recv()
            plane_sum = mine[...]
            for k in range(1, n_rows):
                plane_sum = plane_sum + row_stats[k - 1]
            plane[...] = plane_sum
            for k in range(1, n_tm):
                stat2(k).start()

    for chunk in chunks:
        @pl.when(has_last)
        def _():
            g_copy(2, chunk).wait_recv()

        @pl.when(has_next)
        def _():
            g_copy(1, chunk).start()

        send_rows(1, chunk)

    for k in range(1, n_tm):
        stat2(k).wait_recv()
    whole = plane[...]
    for k in range(1, n_tm):
        whole = whole + tm_stats[k - 1]
    width = channels // GROUPS
    whole = group_total(whole, width) / float(n_tm * n_rows * band * columns * width)
    mean, mean_square = whole[0:1], whole[1:2]
    inverse = lax.rsqrt(mean_square - mean * mean + norm_eps)
    for load in small:
        load.wait()
    scale = inverse * gain[...]
    shift = bias[...] - mean * inverse * gain[...]

    def slot_of(j):
        return j - 2 if 2 <= j < band + 2 else j + band if j < 2 else j

    def hide(frame, j):
        value = ext[frame, band - 2 + j].astype(f32) * scale + shift
        value = 0.5 * value * (1.0 + jnp.tanh(0.5 * value))
        place = r * band + j - 2
        value = jnp.where((place >= 0) & (place < n_rows * band), value, 0.0)
        for i, part in enumerate(side_by_side(value)):
            joined[frame, pl.ds(slot_of(j) * columns, columns), pl.ds(i * channels, channels)] = (
                part.astype(bf16)
            )

    def wait_rows(frame):
        @pl.when(has_below)
        def _():
            for chunk in edge_up:
                r_copy(frame, chunk, 0).wait_recv()

        @pl.when(has_above)
        def _():
            for chunk in edge_down:
                r_copy(frame, chunk, 1).wait_recv()

    def tap(frame, k, first, rows):
        return jnp.dot(
            joined[frame, pl.ds(first * columns, rows * columns), :], w3[frame, k],
            preferred_element_type=f32,
        )

    def own_taps(frame):
        for k in range(3):
            acc[pl.ds((2 - k) * columns, band * columns), :] += tap(frame, k, 0, band)

    def halo_taps(frame):
        acc[pl.ds(0, 2 * columns), :] += tap(frame, 0, band, 2)
        acc[pl.ds(band * columns, 2 * columns), :] += tap(frame, 2, band + 2, 2)
        middle = tap(frame, 1, band + 1, 2)
        acc[pl.ds(0, columns), :] += middle[:columns]
        acc[pl.ds((band + 1) * columns, columns), :] += middle[columns:]

    own = range(2, band + 2)
    halo = [j for j in range(band + 4) if j not in own]

    def hide_rows(frame, rows):
        for j in rows:
            hide(frame, j)

    def older(chunk):
        @pl.when(has_last)
        def _():
            g_copy(1, chunk).wait_recv()

        send_rows(0, chunk)

    acc[...] = jnp.zeros(acc.shape, f32) + b3[...]
    hide_rows(2, own)
    load3.wait()
    own_taps(2)
    for chunk in chunks:
        older(chunk)
    wait_rows(2)
    hide_rows(2, halo)
    halo_taps(2)
    hide_rows(1, own)
    own_taps(1)
    hide_rows(0, own)
    wait_rows(1)
    hide_rows(1, halo)
    halo_taps(1)
    own_taps(0)
    wait_rows(0)
    hide_rows(0, halo)
    halo_taps(0)

    for j in range(band + 2):
        value = ext[2, band - 1 + j].astype(f32) + acc[pl.ds(j * columns, columns), :]
        place = r * band + j - 1
        value = jnp.where((place >= 0) & (place < n_rows * band), value, 0.0)
        for i, part in enumerate(side_by_side(value)):
            mjoined[pl.ds(j * columns, columns), pl.ds(i * channels, channels)] = part.astype(bf16)

    for p in range(2):
        for q in range(2):
            summed = b2[...]
            for t in range(2):
                summed = summed + jnp.dot(
                    mjoined[pl.ds((p + t) * columns, band * columns), pl.ds(q * channels, 2 * channels)],
                    cw[p, t, q], preferred_element_type=f32,
                )
            for i in range(band):
                for lane in range(0, channels, 128):
                    spread[2 * i + p, lane // 128, pl.ds(q, columns, stride=2), :] = (
                        summed[i * columns : (i + 1) * columns, lane : lane + 128]
                    )
        for i in range(band):
            for lane in range(0, channels, 128):
                out[0, 2 * i + p, :, pl.ds(lane, 128)] = spread[2 * i + p, lane // 128].astype(bf16)

    for k in range(1, n_rows):
        stat1(k).wait_send()
    for k in range(1, n_tm):
        stat2(k).wait_send()

    @pl.when(has_next)
    def _():
        for chunk in chunks:
            x_copy(chunk).wait_send()
            g_copy(2, chunk).wait_send()
            g_copy(1, chunk).wait_send()

    @pl.when(has_above)
    def _():
        for frame in range(3):
            for chunk in edge_up:
                r_copy(frame, chunk, 0).wait_send()

    @pl.when(has_below)
    def _():
        for frame in range(3):
            for chunk in edge_down:
                r_copy(frame, chunk, 1).wait_send()


def body(
    frames, frame_counts, norm_gain, norm_bias, conv3_weight, conv3_bias, conv2_weight, conv2_bias
):
    n_tm, n_rows = lax.axis_size("tm"), lax.axis_size("rows")
    _, band, columns, channels = frames.shape
    vmem = pl.BlockSpec(memory_space=pltpu.VMEM)
    hbm = pl.BlockSpec(memory_space=pltpu.HBM)
    dma = pltpu.SemaphoreType.DMA
    return pl.pallas_call(
        functools.partial(kernel, n_tm, n_rows),
        out_shape=pltpu.VMEM((1, 2 * band, 2 * columns, channels), bf16),
        in_specs=[
            hbm
        ] * 8,
        out_specs=vmem,
        scratch_shapes=[
            pltpu.SMEM((n_tm,), jnp.int32),
            pltpu.VMEM(frames.shape, bf16),
            pltpu.VMEM((1, channels), f32),
            pltpu.VMEM((1, channels), f32),
            pltpu.VMEM((1, channels), f32),
            pltpu.VMEM((1, channels), f32),
            pltpu.VMEM((3, 3, 3 * channels, channels), bf16),
            pltpu.VMEM((3, 3, channels, channels), bf16),
            pltpu.VMEM((2, 2, 2, 2 * channels, channels), bf16),
            pltpu.VMEM((band, columns, channels), bf16),
            pltpu.VMEM((band, columns, channels), bf16),
            pltpu.VMEM((3, 3 * band, columns, channels), bf16),
            pltpu.VMEM((3, (band + 4) * columns, 3 * channels), bf16),
            pltpu.VMEM(((band + 2) * columns, channels), f32),
            pltpu.VMEM(((band + 2) * columns, 3 * channels), bf16),
            pltpu.VMEM((2 * band, channels // 128, 2 * columns, 128), f32),
            pltpu.VMEM((2, channels), f32),
            pltpu.VMEM((n_rows - 1, 2, channels), f32),
            pltpu.VMEM((2, channels), f32),
            pltpu.VMEM((n_tm - 1, 2, channels), f32),
            dma((8,)),
            dma((HALVES * band,)), dma((HALVES * band,)),
            dma((2, HALVES * band)), dma((2, HALVES * band)),
            dma((3, HALVES * band, 2)), dma((3, HALVES * band, 2)),
            dma((n_rows - 1,)), dma((n_rows - 1,)),
            dma((n_tm - 1,)), dma((n_tm - 1,)),
        ],
        compiler_params=pltpu.CompilerParams(
            collective_id=0, has_side_effects=True, vmem_limit_bytes=60000000
        ),
        name="decoder_section",
    )(
        frame_counts, frames, norm_gain[None], norm_bias[None],
        conv3_weight.reshape(3, 3, 3 * channels, channels), conv3_bias[None],
        conv2_weight, conv2_bias[None],
    )


def solution(mesh):
    placed = (P("tm", "rows", None, None), P(), P(), P(), P(), P(), P(), P())
    return jax.shard_map(
        body, mesh=mesh, in_specs=placed, out_specs=P("tm", "rows", None, None), check_vma=False
    )
```
